32 devices in a mesh: fsdp: 4 (over y, x), context: 2 (over core), tensor: 4 (over z).
Axes of the slice: x: 2, y: 2, z: 4, core: 2. Of those that a mesh axis runs over, the one named last changes fastest.
Arguments:
- tokens: bfloat16 [2048, 640], P(('fsdp', 'context')), may hold values from -16 to 16
- lengths: int32 [4, 4], P('fsdp'), may hold values from 1 to 256, 512 in all within a row
- weight_query: bfloat16 [640, 1024], P('fsdp', 'tensor'), may hold values from -1 to 1
- weight_key: bfloat16 [640, 256], P('fsdp'), may hold values from -1 to 1
- weight_value: bfloat16 [640, 256], P('fsdp'), may hold values from -0.25 to 0.25
- weight_out: bfloat16 [1024, 640], P('tensor', 'fsdp'), may hold values from -0.1875 to 0.1875
- weight_gate: bfloat16 [640, 2048], P('fsdp', 'tensor'), may hold values from -0.25 to 0.25
- weight_up: bfloat16 [640, 2048], P('fsdp', 'tensor'), may hold values from -0.25 to 0.25
- weight_down: bfloat16 [2048, 640], P('tensor', 'fsdp'), may hold values from -0.125 to 0.125
- gain_attn_in: bfloat16 [640], P('fsdp'), may hold values from 0.099609375 to 1.8984375
- gain_attn_out: bfloat16 [640], P('fsdp'), may hold values from 0.099609375 to 1.8984375
- gain_ffn_in: bfloat16 [640], P('fsdp'), may hold values from 0.099609375 to 1.8984375
- gain_ffn_out: bfloat16 [640], P('fsdp'), may hold values from 0.099609375 to 1.8984375
- gain_query: bfloat16 [256], P('fsdp'), may hold values from 0.5 to 2
- gain_key: bfloat16 [256], P('fsdp'), may hold values from 0.5 to 2
- cotangent: bfloat16 [2048, 640], P(('fsdp', 'context')), may hold values from -6 to 6
Outputs:
- layer_output: float32 [2048, 640], P(('fsdp', 'context'))
- grad_input: float32 [2048, 640], P(('fsdp', 'context'))
- grad_weight_query: float32 [640, 1024], P('fsdp', 'tensor')
- grad_weight_key: float32 [640, 256], P('fsdp')
- grad_weight_value: float32 [640, 256], P('fsdp')
- grad_weight_out: float32 [1024, 640], P('tensor', 'fsdp')
- grad_weight_gate: float32 [640, 2048], P('fsdp', 'tensor')
- grad_weight_up: float32 [640, 2048], P('fsdp', 'tensor')
- grad_weight_down: float32 [2048, 640], P('tensor', 'fsdp')
- grad_gain_attn_in: float32 [640], P('fsdp')
- grad_gain_attn_out: float32 [640], P('fsdp')
- grad_gain_ffn_in: float32 [640], P('fsdp')
- grad_gain_ffn_out: float32 [640], P('fsdp')
- grad_gain_query: float32 [256], P('fsdp')
- grad_gain_key: float32 [256], P('fsdp')
The draws below stay inside these ranges and needn't reach their ends.
Inputs may be any that keep to these rules, and one draw needn't show every extreme that they name: `lengths`: each row sums to 512; its largest entry is exactly 256.
All inputs are finite; a program needn't handle non-finite values.
Results may differ from the reference program's by a relative error of at most 0.015.
Values may be sent and summed in bfloat16 or wider, within the bound.
No kernel may reach another device: no remote copies, remote signals or barrier semaphores. Data moves between devices by JAX's collectives and lax.ppermute only.
A program may use at most 128 MiB of HBM per device.

```python
import math
import jax
import jax.numpy as jnp
import numpy as np
from jax import lax

D = 640
HEADS = 4
HD = 256
FF = 2048
GROUP = 256
NSEQ = 4
STREAM = 512
TOKENS = 2048
N_FSDP = 4
N_CONTEXT = 2


def draw_tokens(key, part):
    noise = jnp.clip(jax.random.normal(jax.random.fold_in(key, 3), (TOKENS, D), jnp.float32), -6.0, 6.0)
    return noise.astype(jnp.bfloat16)


def query_matrix(key):
    fresh = jnp.clip(jax.random.normal(jax.random.fold_in(key, 11), (D, HEADS * HD), jnp.float32), -6.0, 6.0)
    return fresh * D ** (-0.5)


def draw_weight_query(key, part):
    return query_matrix(key).astype(jnp.bfloat16)


def draw_weight_key(key, part):
    return (jnp.clip(jax.random.normal(jax.random.fold_in(key, 12), (D, HD), jnp.float32), -6.0, 6.0) * D ** (-0.5)).astype(jnp.bfloat16)


def draw_gain_query(key, part):
    return jnp.clip(1.25 + 0.3 * jax.random.normal(jax.random.fold_in(key, 21), (HD,), jnp.float32), 0.5, 2.0).astype(jnp.bfloat16)


def draw_gain_key(key, part):
    return jnp.clip(1.25 + 0.3 * jax.random.normal(jax.random.fold_in(key, 22), (HD,), jnp.float32), 0.5, 2.0).astype(jnp.bfloat16)


def shard_levels(stream_key, shape, split, least, high):
    factor_of, own = 1.0, jax.random.fold_in(stream_key, 6)
    for dim, shards_of in split:
        steps = jnp.exp(jax.random.uniform(jax.random.fold_in(own, dim), (shards_of,), jnp.float32, least / len(split), high / len(split)))
        factor_of = factor_of * jnp.repeat(steps, shape[dim] // shards_of).reshape([-1 if axis == dim else 1 for axis in range(len(shape))])
    return factor_of


def profile(count, total, most, lean):
    weights = [(1 << 20) // math.isqrt(standing ** lean) + 1 for standing in range(2, count + 1)]
    surplus, counts = total - most - (count - 1), [1] * (count - 1)
    while surplus > 0:
        free = [i for i in range(count - 1) if counts[i] < most]
        whole, budget = sum([weights[i] for i in free]), surplus
        for i in free:
            more = min(most - counts[i], max(1, budget * weights[i] // whole), surplus)
            counts[i] = counts[i] + more
            surplus = surplus - more
    return np.array([most] + counts)


def ragged_sizes(key, number_of, total, reach, lean):
    if number_of == 2:
        one = jax.random.randint(key, (), max(1, total - reach), min(reach, total - 1) + 1)
        return jnp.stack([one, total - one])
    sizes = jnp.asarray(profile(number_of, total, reach, lean), jnp.int32)
    couples = (number_of - 1) // 2
    donor, sink = sizes[1:1 + 2 * couples:2], sizes[2:2 + 2 * couples:2]
    room = jnp.minimum(donor - 1, reach - sink)
    moved = jax.random.randint(jax.random.fold_in(key, 1), (couples,), 0, 1 << 20) % (room + 1)
    sizes = sizes.at[1:1 + 2 * couples:2].set(donor - moved).at[2:2 + 2 * couples:2].set(sink + moved)
    return sizes[jax.random.permutation(jax.random.fold_in(key, 2), number_of)]


def centred(stream_key, shape, scale, reach, split=(), kind=jnp.bfloat16):
    gain = shard_levels(stream_key, shape, split, -0.22, 0.18) if split else 1.0
    entries = jax.random.normal(stream_key, shape, jnp.float32) * scale * gain
    return jnp.minimum(jnp.maximum(entries, -reach), reach).astype(kind)


def setup_inputs(seed: int = 0) -> dict:
    key_of = jax.random.split(jax.random.key(seed), 17)
    tokens = draw_tokens(jax.random.fold_in(key_of[16], 71), 0)
    lengths = jax.vmap(lambda own: ragged_sizes(own, NSEQ, STREAM, STREAM // 2, 2))(jax.random.split(key_of[1], N_FSDP)).reshape((N_FSDP, NSEQ)).astype(jnp.int32)
    weight_query = draw_weight_query(jax.random.fold_in(key_of[16], 71), 0)
    weight_key = draw_weight_key(jax.random.fold_in(key_of[16], 71), 0)
    weight_value = centred(key_of[4], (D, HD), D ** -0.5, 0.25, ((0, 4),))
    weight_out = centred(key_of[5], (HEADS * HD, D), (HEADS * HD) ** -0.5, 0.1875, ((0, 4), (1, 4)))
    weight_gate = centred(key_of[6], (D, FF), D ** -0.5, 0.25, ((0, 4), (1, 4)))
    weight_up = centred(key_of[7], (D, FF), D ** -0.5, 0.25, ((0, 4), (1, 4)))
    weight_down = centred(key_of[8], (FF, D), FF ** -0.5, 0.125, ((0, 4), (1, 4)))
    gain_attn_in = jnp.clip(1.0 + 0.18 * jax.random.normal(key_of[9], (D,), jnp.float32), 0.099609375, 1.8984375).astype(jnp.bfloat16)
    gain_attn_out = jnp.clip(1.0 + 0.18 * jax.random.normal(key_of[10], (D,), jnp.float32), 0.099609375, 1.8984375).astype(jnp.bfloat16)
    gain_ffn_in = jnp.clip(1.0 + 0.18 * jax.random.normal(key_of[11], (D,), jnp.float32), 0.099609375, 1.8984375).astype(jnp.bfloat16)
    gain_ffn_out = jnp.clip(1.0 + 0.18 * jax.random.normal(key_of[12], (D,), jnp.float32), 0.099609375, 1.8984375).astype(jnp.bfloat16)
    gain_query = draw_gain_query(jax.random.fold_in(key_of[16], 71), 0)
    gain_key = draw_gain_key(jax.random.fold_in(key_of[16], 71), 0)
    cotangent = centred(key_of[15], (TOKENS, D), 1.0, 6.0, ((0, 8),))
    return {"tokens": tokens, "lengths": lengths, "weight_query": weight_query, "weight_key": weight_key, "weight_value": weight_value, "weight_out": weight_out, "weight_gate": weight_gate, "weight_up": weight_up, "weight_down": weight_down, "gain_attn_in": gain_attn_in, "gain_attn_out": gain_attn_out, "gain_ffn_in": gain_ffn_in, "gain_ffn_out": gain_ffn_out, "gain_query": gain_query, "gain_key": gain_key, "cotangent": cotangent}


EPSILON = 1e-06
ROPE_BASE = 1000000.0
GELU_COEF = math.sqrt(2.0 / math.pi)
NEG_LARGE = -1e+30

def to_bf16(values):
    return lax.optimization_barrier(values.astype(jnp.bfloat16))

def rms_forward(values, gain_vec):
    inverse = lax.rsqrt(lax.optimization_barrier(jnp.mean(values * values, axis=-1, keepdims=True)) + EPSILON)
    normed = values * inverse
    return (normed * gain_vec, normed, inverse)

def rms_backward(grad_out, gain_vec, normed, inverse):
    gain_grad = lax.optimization_barrier(jnp.sum(grad_out * normed, axis=tuple(range(grad_out.ndim - 1))))
    inner = grad_out * gain_vec
    grad_in = inverse * (inner - normed * lax.optimization_barrier(jnp.mean(inner * normed, axis=-1, keepdims=True)))
    return (grad_in, gain_grad)

def rope_tables(positions, width):
    half_width = width // 2
    freqs = ROPE_BASE ** (-jnp.arange(half_width, dtype=jnp.float32) * 2.0 / width)
    angles = positions.astype(jnp.float32)[:, None] * freqs[None, :]
    return (jnp.cos(angles)[:, None, :], jnp.sin(angles)[:, None, :])

def rotate(values, cosine, sine):
    half_width = values.shape[-1] // 2
    first_half = values[..., :half_width]
    second_half = values[..., half_width:]
    return jnp.concatenate([first_half * cosine - second_half * sine, second_half * cosine + first_half * sine], axis=-1)

def rotate_back(values, cosine, sine):
    half_width = values.shape[-1] // 2
    first_half = values[..., :half_width]
    second_half = values[..., half_width:]
    return jnp.concatenate([first_half * cosine + second_half * sine, second_half * cosine - first_half * sine], axis=-1)

def gelu_parts(pre_act):
    cubic = pre_act + 0.044715 * pre_act * pre_act * pre_act
    tangent = jnp.tanh(GELU_COEF * cubic)
    gelu_val = 0.5 * pre_act * (1.0 + tangent)
    slope = 0.5 * (1.0 + tangent) + 0.5 * pre_act * (1.0 - tangent * tangent) * GELU_COEF * (1.0 + 3.0 * 0.044715 * pre_act * pre_act)
    return (gelu_val, slope)

def doc_info(positions, doc_lengths):
    doc_ends = jnp.cumsum(doc_lengths)
    passed = positions[:, None] >= doc_ends[None, :]
    segment = lax.optimization_barrier(jnp.sum(passed.astype(jnp.int32), axis=1))
    doc_start = lax.optimization_barrier(jnp.sum(jnp.where(passed, doc_lengths[None, :], 0), axis=1))
    return (segment, positions - doc_start)

def attention_forward(query_rot, key_rot, value_own, segment, token_index):
    total_rows = key_rot.shape[0]
    blk_rows = math.gcd(total_rows, 512)
    key_float = key_rot.astype(jnp.float32)
    value_float = value_own.astype(jnp.float32)

    def one_block(block_num):
        row_begin = block_num * blk_rows
        query_blk = lax.dynamic_slice_in_dim(query_rot, row_begin, blk_rows, 0).astype(jnp.float32)
        seg_blk = lax.dynamic_slice_in_dim(segment, row_begin, blk_rows, 0)
        idx_blk = lax.dynamic_slice_in_dim(token_index, row_begin, blk_rows, 0)
        allowed = (seg_blk[:, None] == segment[None, :]) & (idx_blk[:, None] >= token_index[None, :])
        scores = jnp.einsum('qhd,kd->hqk', query_blk, key_float)
        scores = jnp.where(allowed[None], scores, NEG_LARGE)
        row_max = lax.optimization_barrier(jnp.max(scores, axis=2))
        weights = jnp.where(allowed[None], jnp.exp(scores - row_max[:, :, None]), 0.0)
        totals = lax.optimization_barrier(jnp.sum(weights, axis=2))
        rounded = to_bf16(weights).astype(jnp.float32)
        summed = jnp.einsum('hqk,kd->qhd', rounded, value_float)
        return (summed / totals.T[:, :, None], (row_max + jnp.log(totals)).T)
    results, log_totals = lax.map(one_block, jnp.arange(total_rows // blk_rows, dtype=jnp.int32))
    return (results.reshape(total_rows, HEADS, HD), log_totals.reshape(total_rows, HEADS))

def attention_backward(query_rot, key_rot, value_own, grad_heads, log_total, delta, segment, token_index):
    total_rows = key_rot.shape[0]
    blk_rows = math.gcd(total_rows, 512)
    key_float = key_rot.astype(jnp.float32)
    value_float = value_own.astype(jnp.float32)

    def one_block(carry, block_num):
        key_acc, value_acc = carry
        row_begin = block_num * blk_rows
        query_blk = lax.dynamic_slice_in_dim(query_rot, row_begin, blk_rows, 0).astype(jnp.float32)
        grad_blk = lax.dynamic_slice_in_dim(grad_heads, row_begin, blk_rows, 0).astype(jnp.float32)
        lse_blk = lax.dynamic_slice_in_dim(log_total, row_begin, blk_rows, 0)
        delta_blk = lax.dynamic_slice_in_dim(delta, row_begin, blk_rows, 0)
        seg_blk = lax.dynamic_slice_in_dim(segment, row_begin, blk_rows, 0)
        idx_blk = lax.dynamic_slice_in_dim(token_index, row_begin, blk_rows, 0)
        allowed = (seg_blk[:, None] == segment[None, :]) & (idx_blk[:, None] >= token_index[None, :])
        scores = jnp.einsum('qhd,kd->hqk', query_blk, key_float)
        probs = jnp.where(allowed[None], jnp.exp(scores - lse_blk.T[:, :, None]), 0.0)
        grad_probs = jnp.einsum('qhd,kd->hqk', grad_blk, value_float)
        grad_scores = probs * (grad_probs - delta_blk.T[:, :, None])
        scores_round = to_bf16(grad_scores).astype(jnp.float32)
        probs_round = to_bf16(probs).astype(jnp.float32)
        grad_query = jnp.einsum('hqk,kd->qhd', scores_round, key_float)
        key_acc = key_acc + jnp.einsum('hqk,qhd->kd', scores_round, query_blk)
        value_acc = value_acc + jnp.einsum('hqk,qhd->kd', probs_round, grad_blk)
        return ((key_acc, value_acc), grad_query)
    zero_rows = jnp.zeros((total_rows, HD), jnp.float32)
    (key_grad, value_grad), grad_query = lax.scan(one_block, (zero_rows, zero_rows), jnp.arange(total_rows // blk_rows, dtype=jnp.int32))
    return (grad_query.reshape(total_rows, HEADS, HD), key_grad, value_grad)

def dot32(mat_left, mat_right):
    return jnp.dot(mat_left, mat_right, preferred_element_type=jnp.float32)

def layer_stream(tok_stream, doc_lengths, cot_stream, weights, gains):
    weight_query, weight_key, weight_value, weight_out, weight_gate, weight_up, weight_down = weights
    scale_ai, scale_ao, scale_fi, scale_fo, scale_q, scale_k = gains
    total_rows = tok_stream.shape[0]
    token_index = jnp.arange(total_rows, dtype=jnp.int32)
    segment, position = doc_info(token_index, doc_lengths)
    cosine, sine = rope_tables(position, HD)
    att_scale = HD ** (-0.5)
    inputs_f = tok_stream.astype(jnp.float32)
    normed_one, hat_one, inv_one = rms_forward(inputs_f, scale_ai)
    act_one = to_bf16(normed_one)
    query_pre = dot32(act_one, weight_query).reshape(total_rows, HEADS, HD)
    query_norm, query_hat, query_inv = rms_forward(query_pre, scale_q)
    query_rot = to_bf16(rotate(query_norm, cosine, sine) * att_scale)
    key_pre = dot32(act_one, weight_key).reshape(total_rows, 1, HD)
    key_norm, key_hat, key_inv = rms_forward(key_pre, scale_k)
    key_rot = to_bf16(rotate(key_norm, cosine, sine).reshape(total_rows, HD))
    value_own = to_bf16(dot32(act_one, weight_value))
    attn_float, log_total = attention_forward(query_rot, key_rot, value_own, segment, token_index)
    attn_heads = to_bf16(attn_float)
    attn_cat = attn_heads.reshape(total_rows, HEADS * HD)
    attn_total = dot32(attn_cat, weight_out)
    normed_two, hat_two, inv_two = rms_forward(attn_total, scale_ao)
    hidden_res = inputs_f + normed_two
    normed_three, hat_three, inv_three = rms_forward(hidden_res, scale_fi)
    act_three = to_bf16(normed_three)
    gate_pre = dot32(act_three, weight_gate)
    up_pre = dot32(act_three, weight_up)
    gelu_val, gelu_slope = gelu_parts(gate_pre)
    inner_act = to_bf16(gelu_val * up_pre)
    ffn_total = dot32(inner_act, weight_down)
    normed_four, hat_four, inv_four = rms_forward(ffn_total, scale_fo)
    layer_out = hidden_res + normed_four
    grad_final = cot_stream.astype(jnp.float32)
    grad_ffn, dscale_fo = rms_backward(grad_final, scale_fo, hat_four, inv_four)
    grad_ffn_b = to_bf16(grad_ffn)
    dweight_down = dot32(inner_act.T, grad_ffn_b)
    grad_inner = dot32(grad_ffn_b, weight_down.T)
    grad_gate_b = to_bf16(grad_inner * up_pre * gelu_slope)
    grad_up_b = to_bf16(grad_inner * gelu_val)
    dweight_gate = dot32(act_three.T, grad_gate_b)
    dweight_up = dot32(act_three.T, grad_up_b)
    grad_act_three = dot32(grad_gate_b, weight_gate.T) + dot32(grad_up_b, weight_up.T)
    grad_three, dscale_fi = rms_backward(grad_act_three, scale_fi, hat_three, inv_three)
    grad_hidden = grad_final + grad_three
    grad_attn, dscale_ao = rms_backward(grad_hidden, scale_ao, hat_two, inv_two)
    grad_attn_b = to_bf16(grad_attn)
    dweight_out = dot32(attn_cat.T, grad_attn_b)
    grad_heads = to_bf16(dot32(grad_attn_b, weight_out.T)).reshape(total_rows, HEADS, HD)
    delta = lax.optimization_barrier(jnp.sum(grad_heads.astype(jnp.float32) * attn_heads.astype(jnp.float32), axis=2))
    grad_query_rot, grad_key_rot, grad_value = attention_backward(query_rot, key_rot, value_own, grad_heads, log_total, delta, segment, token_index)
    grad_qnorm = rotate_back(grad_query_rot * att_scale, cosine, sine)
    grad_qpre, dscale_q = rms_backward(grad_qnorm, scale_q, query_hat, query_inv)
    grad_qpre_b = to_bf16(grad_qpre.reshape(total_rows, HEADS * HD))
    grad_knorm = rotate_back(grad_key_rot.reshape(total_rows, 1, HD), cosine, sine)
    grad_kpre, dscale_k = rms_backward(grad_knorm, scale_k, key_hat, key_inv)
    grad_kpre_b = to_bf16(grad_kpre.reshape(total_rows, HD))
    grad_value_b = to_bf16(grad_value)
    dweight_query = dot32(act_one.T, grad_qpre_b)
    dweight_key = dot32(act_one.T, grad_kpre_b)
    dweight_value = dot32(act_one.T, grad_value_b)
    grad_act_one = dot32(grad_qpre_b, weight_query.T) + dot32(grad_kpre_b, weight_key.T) + dot32(grad_value_b, weight_value.T)
    grad_one, dscale_ai = rms_backward(grad_act_one, scale_ai, hat_one, inv_one)
    grad_tokens = grad_hidden + grad_one
    outputs = (layer_out, grad_tokens)
    grads = (dweight_query, dweight_key, dweight_value, dweight_out, dweight_gate, dweight_up, dweight_down, dscale_ai, dscale_ao, dscale_fi, dscale_fo, dscale_q, dscale_k)
    return (outputs, grads)

def reference(tokens, lengths, weight_query, weight_key, weight_value, weight_out, weight_gate, weight_up, weight_down, gain_attn_in, gain_attn_out, gain_ffn_in, gain_ffn_out, gain_query, gain_key, cotangent):
    weights = (weight_query, weight_key, weight_value, weight_out, weight_gate, weight_up, weight_down)
    gain_list = (gain_attn_in, gain_attn_out, gain_ffn_in, gain_ffn_out, gain_query, gain_key)
    gains = tuple((gain_item.astype(jnp.float32) for gain_item in gain_list))
    stream_len = GROUP * N_CONTEXT

    def per_stream(carry, stream_inputs):
        tok_stream, doc_lengths, cot_stream = stream_inputs
        outputs, grads = layer_stream(tok_stream, doc_lengths, cot_stream, weights, gains)
        return (tuple((acc_item + grad_item for acc_item, grad_item in zip(carry, grads))), outputs)
    start_grads = tuple((jnp.zeros(param.shape, jnp.float32) for param in weights + gain_list))
    grads, (outputs, grad_tokens) = lax.scan(per_stream, start_grads, (tokens.reshape(N_FSDP, stream_len, D), lengths, cotangent.reshape(N_FSDP, stream_len, D)))
    return (outputs.reshape(N_FSDP * stream_len, D), grad_tokens.reshape(N_FSDP * stream_len, D), grads[0], grads[1], grads[2], grads[3], grads[4], grads[5], grads[6], grads[7], grads[8], grads[9], grads[10], grads[11], grads[12])
```

```python
import math

import jax
import jax.numpy as jnp
from jax import lax
from jax.sharding import PartitionSpec as P

HD = 256


EPSILON = 1e-06
ROPE_BASE = 1000000.0
GELU_COEF = math.sqrt(2.0 / math.pi)
NEG_LARGE = -1e30


def rms_forward(values, gain_vec):
    inverse = lax.rsqrt(jnp.mean(values * values, axis=-1, keepdims=True) + EPSILON)
    normed = values * inverse
    return (normed * gain_vec, normed, inverse)


def rms_backward(grad_out, gain_vec, normed, inverse):
    gain_grad = jnp.sum(grad_out * normed, axis=tuple(range(grad_out.ndim - 1)))
    inner = grad_out * gain_vec
    grad_in = inverse * (inner - normed * jnp.mean(inner * normed, axis=-1, keepdims=True))
    return (grad_in, gain_grad)


def rope_tables(positions, width):
    half_width = width // 2
    freqs = ROPE_BASE ** (-jnp.arange(half_width, dtype=jnp.float32) * 2.0 / width)
    angles = positions.astype(jnp.float32)[:, None] * freqs[None, :]
    return (jnp.cos(angles)[:, None, :], jnp.sin(angles)[:, None, :])


def rotate(values, cosine, sine):
    half_width = values.shape[-1] // 2
    first_half = values[..., :half_width]
    second_half = values[..., half_width:]
    return jnp.concatenate(
        [first_half * cosine - second_half * sine, second_half * cosine + first_half * sine],
        axis=-1,
    )


def rotate_back(values, cosine, sine):
    half_width = values.shape[-1] // 2
    first_half = values[..., :half_width]
    second_half = values[..., half_width:]
    return jnp.concatenate(
        [first_half * cosine + second_half * sine, second_half * cosine - first_half * sine],
        axis=-1,
    )


def gelu_parts(pre_act):
    cubic = pre_act + 0.044715 * pre_act * pre_act * pre_act
    tangent = jnp.tanh(GELU_COEF * cubic)
    gelu_val = 0.5 * pre_act * (1.0 + tangent)
    slope = 0.5 * (1.0 + tangent) + 0.5 * pre_act * (1.0 - tangent * tangent) * GELU_COEF * (
        1.0 + 3.0 * 0.044715 * pre_act * pre_act
    )
    return (gelu_val, slope)


def doc_info(positions, doc_lengths):
    doc_ends = jnp.cumsum(doc_lengths)
    passed = positions[:, None] >= doc_ends[None, :]
    segment = jnp.sum(passed.astype(jnp.int32), axis=1)
    doc_start = jnp.sum(jnp.where(passed, doc_lengths[None, :], 0), axis=1)
    return (segment, positions - doc_start)


def dot32(mat_left, mat_right):
    return jnp.dot(mat_left, mat_right, preferred_element_type=jnp.float32)


def contract_last(mat_left, mat_right):
    return lax.dot_general(
        mat_left, mat_right, (((1,), (1,)), ((), ())), preferred_element_type=jnp.float32
    )


def contract_first(mat_left, mat_right):
    return lax.dot_general(
        mat_left, mat_right, (((0,), (0,)), ((), ())), preferred_element_type=jnp.float32
    )


def shift_by(values, axis_name, steps):
    count = lax.axis_size(axis_name)
    return lax.ppermute(values, axis_name, [(i, (i + steps) % count) for i in range(count)])


def take_block(blocks, index):
    return lax.dynamic_index_in_dim(blocks, index, 0, keepdims=False)


def scatter_sum(blocks, axis_name):
    count = lax.axis_size(axis_name)
    own = lax.axis_index(axis_name)
    sent = blocks.astype(jnp.bfloat16)
    total = take_block(blocks, own).astype(jnp.float32)
    for steps in range(1, count):
        piece = take_block(sent, (own + steps) % count)
        total = total + shift_by(piece, axis_name, steps).astype(jnp.float32)
    return total


def gather_blocks(values, axis_name):
    count = lax.axis_size(axis_name)
    own = lax.axis_index(axis_name)
    joined = jnp.zeros((count,) + values.shape, values.dtype)
    joined = lax.dynamic_update_index_in_dim(joined, values, own, 0)
    for steps in range(1, count):
        moved = shift_by(values, axis_name, steps)
        joined = lax.dynamic_update_index_in_dim(joined, moved, (own - steps) % count, 0)
    return joined


def scatter_rows(values, axis_name):
    count = lax.axis_size(axis_name)
    return scatter_sum(values.reshape((count, values.shape[0] // count) + values.shape[1:]), axis_name)


def gather_rows(values, axis_name):
    joined = gather_blocks(values, axis_name)
    return joined.reshape((joined.shape[0] * joined.shape[1],) + joined.shape[2:])


def fetch_weights(shard):
    n_context = lax.axis_size("context")
    part_rows = shard.shape[0] // n_context
    part = lax.dynamic_slice_in_dim(shard, lax.axis_index("context") * part_rows, part_rows, 0)
    over_fsdp = gather_blocks(part, "fsdp")
    joined = jnp.swapaxes(lax.all_gather(over_fsdp, "context", axis=0, tiled=False), 0, 1)
    return over_fsdp, joined.reshape(-1, shard.shape[1])


def reduce_grads(grad):
    n_context = lax.axis_size("context")
    n_fsdp = lax.axis_size("fsdp")
    rows, cols = grad.shape
    parts = grad.reshape(n_fsdp, n_context, rows // (n_fsdp * n_context), cols)
    mine = scatter_sum(jnp.swapaxes(parts, 0, 1), "context")
    mine = scatter_sum(mine, "fsdp")
    return lax.all_gather(mine, "context", axis=0, tiled=True)


def on_device(
    tokens,
    lengths,
    weight_query,
    weight_key,
    weight_value,
    weight_out,
    weight_gate,
    weight_up,
    weight_down,
    gain_attn_in,
    gain_attn_out,
    gain_ffn_in,
    gain_ffn_out,
    gain_query,
    gain_key,
    cotangent,
):
    group_rows, width = tokens.shape
    n_context = lax.axis_size("context")
    n_tensor = lax.axis_size("tensor")
    stream_len = group_rows * n_context
    q_cols = weight_query.shape[1]
    ff_cols = weight_gate.shape[1]
    heads_here = q_cols // HD
    query_count = heads_here * group_rows
    own_rows = group_rows // n_tensor
    row_begin = lax.axis_index("tensor") * own_rows

    def my_rows(values):
        return lax.dynamic_slice_in_dim(values, row_begin, own_rows, 0)

    gains = gather_blocks(
        jnp.concatenate(
            [gain_attn_in, gain_attn_out, gain_ffn_in, gain_ffn_out, gain_query, gain_key]
        ),
        "fsdp",
    ).astype(jnp.float32)
    sizes = [gain_attn_in.shape[0]] * 4 + [gain_query.shape[0]] * 2
    scales, begin = [], 0
    for size in sizes:
        scales.append(gains[:, begin : begin + size].reshape(-1))
        begin += size
    scale_ai, scale_ao, scale_fi, scale_fo, scale_q, scale_k = scales

    first_part, full_qkv = fetch_weights(
        jnp.concatenate([weight_query, weight_key, weight_value], axis=1)
    )
    second_in = jnp.concatenate([weight_out.T, weight_gate, weight_up, weight_down.T], axis=1)
    second_in, first_part = lax.optimization_barrier((second_in, first_part))
    full_second = fetch_weights(second_in)[1]
    full_query = full_qkv[:, :q_cols]
    full_kv = full_qkv[:, q_cols:]
    full_out_t = full_second[:, :q_cols]
    full_gate_up = full_second[:, q_cols : q_cols + 2 * ff_cols]
    full_down_t = full_second[:, q_cols + 2 * ff_cols :]

    doc_lengths = lengths[0]
    own_index = lax.axis_index("context") * group_rows + jnp.arange(group_rows, dtype=jnp.int32)
    own_segment, own_position = doc_info(own_index, doc_lengths)
    cosine, sine = rope_tables(own_position, HD)
    row_segment = jnp.tile(own_segment, heads_here)
    row_index = jnp.tile(own_index, heads_here)
    att_scale = HD ** (-0.5)
    inputs_f = tokens.astype(jnp.float32)
    normed_one = rms_forward(inputs_f, scale_ai)[0]
    act_one = normed_one.astype(jnp.bfloat16)
    inputs_mine = my_rows(inputs_f)
    hat_one, inv_one = rms_forward(inputs_mine, scale_ai)[1:]
    qkv_pre = dot32(act_one, full_qkv)
    query_pre = qkv_pre[:, :q_cols].reshape(group_rows, heads_here, HD)
    query_norm, query_hat, query_inv = rms_forward(query_pre, scale_q)
    query_rot = (rotate(query_norm, cosine, sine) * att_scale).astype(jnp.bfloat16)
    query_rows = jnp.transpose(query_rot, (1, 0, 2)).reshape(query_count, HD)
    key_pre = qkv_pre[:, q_cols : q_cols + HD].reshape(group_rows, 1, HD)
    key_norm = rms_forward(key_pre, scale_k)[0]
    key_hat, key_inv = rms_forward(my_rows(key_pre), scale_k)[1:]
    key_rot = rotate(key_norm, cosine, sine).reshape(group_rows, HD).astype(jnp.bfloat16)
    value_own = qkv_pre[:, q_cols + HD :].astype(jnp.bfloat16)

    key_value = lax.all_gather(
        jnp.concatenate([key_rot, value_own], axis=1), "context", axis=0, tiled=True
    )
    key_all = key_value[:, :HD]
    value_all = key_value[:, HD:]
    key_index = jnp.arange(stream_len, dtype=jnp.int32)
    key_segment = doc_info(key_index, doc_lengths)[0]
    allowed = (row_segment[:, None] == key_segment[None, :]) & (
        row_index[:, None] >= key_index[None, :]
    )
    scores = jnp.where(allowed, contract_last(query_rows, key_all), NEG_LARGE)
    run_max = jnp.max(scores, axis=1)
    weights = jnp.where(allowed, jnp.exp(scores - run_max[:, None]), 0.0)
    run_sum = jnp.sum(weights, axis=1)
    run_acc = dot32(weights.astype(jnp.bfloat16), value_all)
    out_rows = (run_acc / run_sum[:, None]).astype(jnp.bfloat16)
    attn_cat = jnp.transpose(out_rows.reshape(heads_here, group_rows, HD), (1, 0, 2)).reshape(
        group_rows, q_cols
    )
    attn_total = scatter_rows(contract_last(attn_cat, full_out_t), "tensor")
    normed_two, hat_two, inv_two = rms_forward(attn_total, scale_ao)
    hidden_res = inputs_mine + normed_two
    normed_three, hat_three, inv_three = rms_forward(hidden_res, scale_fi)
    act_three = gather_rows(normed_three.astype(jnp.bfloat16), "tensor")
    gate_up = dot32(act_three, full_gate_up)
    gate_pre = gate_up[:, :ff_cols]
    up_pre = gate_up[:, ff_cols:]
    gelu_val, gelu_slope = gelu_parts(gate_pre)
    inner_act = (gelu_val * up_pre).astype(jnp.bfloat16)
    ffn_total = scatter_rows(contract_last(inner_act, full_down_t), "tensor")
    normed_four, hat_four, inv_four = rms_forward(ffn_total, scale_fo)
    layer_mine = hidden_res + normed_four
    grad_final = my_rows(cotangent).astype(jnp.float32)
    grad_ffn, dscale_fo = rms_backward(grad_final, scale_fo, hat_four, inv_four)
    grad_ffn_b = gather_rows(grad_ffn.astype(jnp.bfloat16), "tensor")
    grad_inner = dot32(grad_ffn_b, full_down_t)
    grad_gate_b = (grad_inner * up_pre * gelu_slope).astype(jnp.bfloat16)
    grad_up_b = (grad_inner * gelu_val).astype(jnp.bfloat16)
    grad_gate_up = jnp.concatenate([grad_gate_b, grad_up_b], axis=1)
    grad_act_three = scatter_rows(contract_last(grad_gate_up, full_gate_up), "tensor")
    layer_out = gather_rows(layer_mine.astype(jnp.bfloat16), "tensor").astype(jnp.float32)
    ffn_shares = reduce_grads(
        jnp.concatenate(
            [contract_first(act_three, grad_gate_up), contract_first(grad_ffn_b, inner_act)],
            axis=1,
        )
    )
    grad_three, dscale_fi = rms_backward(grad_act_three, scale_fi, hat_three, inv_three)
    grad_hidden = grad_final + grad_three
    grad_attn, dscale_ao = rms_backward(grad_hidden, scale_ao, hat_two, inv_two)
    grad_attn_b = gather_rows(grad_attn.astype(jnp.bfloat16), "tensor")
    grad_cat = dot32(grad_attn_b, full_out_t).astype(jnp.bfloat16)
    grad_rows = jnp.transpose(grad_cat.reshape(group_rows, heads_here, HD), (1, 0, 2)).reshape(
        query_count, HD
    )
    delta_rows = jnp.sum(grad_rows.astype(jnp.float32) * out_rows.astype(jnp.float32), axis=1)
    probs = weights / run_sum[:, None]
    grad_probs = contract_last(grad_rows, value_all)
    grad_scores_b = (probs * (grad_probs - delta_rows[:, None])).astype(jnp.bfloat16)
    grad_query_rows = dot32(grad_scores_b, key_all)
    kv_terms = jnp.concatenate(
        [
            contract_first(grad_scores_b, query_rows),
            contract_first(probs.astype(jnp.bfloat16), grad_rows),
        ],
        axis=1,
    )
    kv_mine = scatter_rows(scatter_rows(kv_terms, "context"), "tensor")
    grad_query = jnp.transpose(grad_query_rows.reshape(heads_here, group_rows, HD), (1, 0, 2))
    grad_qnorm = rotate_back(grad_query * att_scale, cosine, sine)
    grad_qpre, dscale_q = rms_backward(grad_qnorm, scale_q, query_hat, query_inv)
    grad_qpre_b = grad_qpre.reshape(group_rows, q_cols).astype(jnp.bfloat16)
    grad_act_part = scatter_rows(contract_last(grad_qpre_b, full_query), "tensor")
    grad_knorm = rotate_back(
        kv_mine[:, :HD].reshape(own_rows, 1, HD), my_rows(cosine), my_rows(sine)
    )
    grad_kpre, dscale_k = rms_backward(grad_knorm, scale_k, key_hat, key_inv)
    grad_kv_mine = jnp.concatenate(
        [grad_kpre.reshape(own_rows, HD), kv_mine[:, HD:]], axis=1
    ).astype(jnp.bfloat16)
    grad_kv_b = gather_rows(grad_kv_mine, "tensor")
    attn_shares = reduce_grads(
        jnp.concatenate(
            [contract_first(grad_attn_b, attn_cat), contract_first(act_one, grad_qpre_b)],
            axis=1,
        )
    )
    kv_shares = reduce_grads(contract_first(act_one, grad_kv_b))
    grad_act_one = grad_act_part + contract_last(grad_kv_mine, full_kv)
    grad_one, dscale_ai = rms_backward(grad_act_one, scale_ai, hat_one, inv_one)
    grad_tokens = gather_rows((grad_hidden + grad_one).astype(jnp.bfloat16), "tensor").astype(
        jnp.float32
    )
    dscales = lax.psum(
        jnp.concatenate([dscale_ai, dscale_ao, dscale_fi, dscale_fo, dscale_q, dscale_k]),
        ("fsdp", "context", "tensor"),
    )
    gain_shares, begin = [], 0
    n_fsdp = lax.axis_size("fsdp")
    own_fsdp = lax.axis_index("fsdp")
    for size in sizes:
        gain_shares.append(
            lax.dynamic_slice_in_dim(dscales, begin + own_fsdp * size, size, 0)
        )
        begin += n_fsdp * size
    return (
        layer_out,
        grad_tokens,
        attn_shares[:, q_cols:],
        kv_shares[:, :HD],
        kv_shares[:, HD:],
        attn_shares[:, :q_cols].T,
        ffn_shares[:, :ff_cols],
        ffn_shares[:, ff_cols : 2 * ff_cols],
        ffn_shares[:, 2 * ff_cols :].T,
        *gain_shares,
    )


def solution(mesh):
    in_specs = (
        P(("fsdp", "context"), None),
        P("fsdp", None),
        P("fsdp", "tensor"),
        P("fsdp", None),
        P("fsdp", None),
        P("tensor", "fsdp"),
        P("fsdp", "tensor"),
        P("fsdp", "tensor"),
        P("tensor", "fsdp"),
        P("fsdp"),
        P("fsdp"),
        P("fsdp"),
        P("fsdp"),
        P("fsdp"),
        P("fsdp"),
        P(("fsdp", "context"), None),
    )
    out_specs = (
        P(("fsdp", "context"), None),
        P(("fsdp", "context"), None),
        P("fsdp", "tensor"),
        P("fsdp", None),
        P("fsdp", None),
        P("tensor", "fsdp"),
        P("fsdp", "tensor"),
        P("fsdp", "tensor"),
        P("tensor", "fsdp"),
        P("fsdp"),
        P("fsdp"),
        P("fsdp"),
        P("fsdp"),
        P("fsdp"),
        P("fsdp"),
    )
    return jax.shard_map(
        on_device, mesh=mesh, in_specs=in_specs, out_specs=out_specs, check_vma=False
    )
```
